32 devices in a mesh: row: 8 (over y, x, core), col: 4 (over z).
Axes of the slice: x: 2, y: 2, z: 4, core: 2. Of those that a mesh axis runs over, the one named last changes fastest.
Arguments:
- velocity: float32 [3, 2, 128, 256, 256], P(None, None, 'row', 'col'), may hold values from -7.5 to 7.5
- accumulator: float32 [3, 2, 128, 256, 256], P(None, None, 'row', 'col'), may hold values from -6 to 6
- remesh_flag: int32 [128], P('row'), may hold values 0 or 1
- remesh_shift: int32 [128], P('row'), may hold values from -128 to 127
- viscosity: float32 [1], replicated, may hold values from 0.0003 to 0.0015
- shear: float32 [1], replicated, may hold values from 8 to 20
- clock: float32 [1], replicated, may hold values from 0 to 0.05
- step: float32 [1], replicated, may hold values from 0.004 to 0.01
Outputs:
- new_velocity: float32 [3, 2, 128, 256, 256], P(None, None, 'row', 'col')
- new_accumulator: float32 [3, 2, 128, 256, 256], P(None, None, 'row', 'col')
- spectra: float32 [2, 128], P(None, 'row')
The draws below stay inside these ranges and needn't reach their ends.
All inputs are finite; a program needn't handle non-finite values. No bound on the sum of `remesh_flag` on one device may be relied on, other than what follows from the above.
Results may differ from the reference program's by a relative error of at most 0.0001.
Values sent between devices are 32-bit elements; how exact they have to be, the bound alone decides.
A program may use at most 192 MiB of HBM per device.

```python
import math
import jax
import jax.numpy as jnp

NX = 256
NY = 256
NZ = 256
KX = 128


def draw_velocity(key, part):
    first_key = jax.random.fold_in(jax.random.fold_in(key, 11), 0)
    sample = jnp.clip(jax.random.normal(first_key, (3, 2, KX, NZ, NY), jnp.float32), -4.0, 4.0)
    correlated = sample.at[1].add(-0.6 * sample[0])
    return correlated


def set_ends(entries, stream_key, smallest, top_value):
    shape = entries.shape
    spot = [jax.random.randint(jax.random.fold_in(stream_key, axis), (), 0, shape[axis]) for axis in range(len(shape))]
    entries = entries.at[tuple(spot)].set(smallest)
    longest = shape.index(max(shape))
    spot[longest] = (spot[longest] + 1) % shape[longest]
    return entries.at[tuple(spot)].set(top_value)


def block_levels(stream_key, extent, cuts, low, high):
    gain = 1.0
    for position, parts in cuts:
        heights = jax.random.uniform(jax.random.fold_in(jax.random.fold_in(stream_key, 6), position), (parts,), jnp.float32, low / len(cuts), high / len(cuts))
        gain = gain * jnp.repeat(jnp.exp(heights), extent[position] // parts).reshape((-1,) + (1,) * (len(extent) - 1 - position))
    return gain


def gaussian(key, shape, width, bound, cuts=(), held_as=jnp.bfloat16):
    values = width * jax.random.normal(key, shape, jnp.float32)
    if cuts:
        values = values * block_levels(key, shape, cuts, -0.22, 0.18)
    return jnp.clip(values, -bound, bound).astype(held_as)


def setup_inputs(seed: int = 0) -> dict:
    key_list = jax.random.split(jax.random.key(seed), 9)
    return {
        "velocity": draw_velocity(jax.random.fold_in(key_list[8], 71), 0),
        "accumulator": gaussian(key_list[1], (3, 2, KX, NZ, NY), 1.0, 6.0, ((2, 8), (3, 4)), jnp.float32),
        "remesh_flag": set_ends((jax.random.randint(key_list[2], (KX,), 0, 2) < 1).astype(jnp.int32), jax.random.fold_in(key_list[2], 1), 0, 1),
        "remesh_shift": set_ends(jax.random.randint(key_list[3], (KX,), 0 - NY // 2, NY // 2), jax.random.fold_in(key_list[3], 1), 0 - NY // 2, (NY // 2) - 1).astype(jnp.int32),
        "viscosity": jnp.clip(jnp.exp(jax.random.uniform(key_list[4], (1,), jnp.float32, math.log(0.0003), math.log(0.0015))), 0.0003, 0.0015),
        "shear": jnp.clip(jax.random.uniform(key_list[5], (1,), jnp.float32, 8.0, 20.0), 8.0, 20.0),
        "clock": jnp.clip(jax.random.uniform(key_list[6], (1,), jnp.float32, 0.0, 0.05), 0.0, 0.05),
        "step": jnp.clip(jax.random.uniform(key_list[7], (1,), jnp.float32, 0.004, 0.01), 0.004, 0.01),
    }


def signed_index(positions, period):
    return jnp.where(2 * positions < period, positions, positions - period)


def roll_rows(field, amounts):
    def shift_row(row_data, amount_one):
        return jnp.roll(row_data, -amount_one, axis=-1)
    return jax.vmap(shift_row, in_axes=(2, 0), out_axes=2)(field, amounts)


def project(real_part, imag_part, wave_vector, inverse_square):
    along_real = (wave_vector[0] * real_part[0] + wave_vector[1] * real_part[1] + wave_vector[2] * real_part[2]) * inverse_square
    along_imag = (wave_vector[0] * imag_part[0] + wave_vector[1] * imag_part[1] + wave_vector[2] * imag_part[2]) * inverse_square
    return (jnp.stack([real_part[number] - wave_vector[number] * along_real for number in range(3)]),
            jnp.stack([imag_part[number] - wave_vector[number] * along_imag for number in range(3)]))


def cross_product(first_one, second_one):
    return jnp.stack([first_one[1] * second_one[2] - first_one[2] * second_one[1],
                      first_one[2] * second_one[0] - first_one[0] * second_one[2],
                      first_one[0] * second_one[1] - first_one[1] * second_one[0]])


def to_grid(real_part, imag_part):
    weights = jnp.where(jnp.arange(KX) == 0, 1.0, 2.0).astype(jnp.float32)[:, None, None]
    result_list = []
    for number in range(3):
        half = weights * (real_part[number] + 1j * imag_part[number])
        full = jnp.zeros((NX, NZ, NY), half.dtype).at[:KX].set(half)
        result_list.append(jnp.real(jnp.fft.ifftn(full, norm="ortho")))
    return jnp.stack(result_list)


def reference(velocity, accumulator, remesh_flag, remesh_shift, viscosity, shear, clock, step):
    offset = remesh_flag * remesh_shift
    remeshed = roll_rows(velocity, offset)
    carried = roll_rows(accumulator, offset)
    lattice_x = jnp.arange(KX, dtype=jnp.int32)
    lattice_z = signed_index(jnp.arange(NZ, dtype=jnp.int32), NZ)
    lattice_y = signed_index(jnp.arange(NY, dtype=jnp.int32), NY)
    wave_x = lattice_x.astype(jnp.float32)[:, None, None]
    wave_z = lattice_z.astype(jnp.float32)[None, :, None]
    wave_y = lattice_y.astype(jnp.float32)[None, None, :] - shear[0] * clock[0] * wave_x
    wave_vector = (wave_x, wave_y, wave_z)
    square_wave = wave_x * wave_x + wave_y * wave_y + wave_z * wave_z
    inverse_square = 1.0 / jnp.maximum(square_wave, 1.0)
    dealias_mask = ((3 * lattice_x < NX)[:, None, None] & (3 * jnp.abs(lattice_z) < NZ)[None, :, None]
                    & (3 * jnp.abs(lattice_y) < NY)[None, None, :]).astype(jnp.float32)
    solen_real, solen_imag = project(remeshed[:, 0], remeshed[:, 1], wave_vector, inverse_square)
    smooth_real = dealias_mask * solen_real
    smooth_imag = dealias_mask * solen_imag
    vort_real = -cross_product(wave_vector, smooth_imag)
    vort_imag = cross_product(wave_vector, smooth_real)
    flow_grid = to_grid(smooth_real, smooth_imag)
    swirl_grid = to_grid(vort_real, vort_imag)
    lamb_grid = cross_product(flow_grid, swirl_grid)
    lamb_hat = [jnp.fft.fftn(lamb_grid[number], norm="ortho")[:KX] for number in range(3)]
    hat_real = dealias_mask * jnp.stack([jnp.real(spectrum) for spectrum in lamb_hat])
    hat_imag = dealias_mask * jnp.stack([jnp.imag(spectrum) for spectrum in lamb_hat])
    proj_real, proj_imag = project(hat_real, hat_imag, wave_vector, inverse_square)
    shear_rate = shear[0]
    viscous_rate = viscosity[0]
    coupling = 2.0 * shear_rate * wave_x * inverse_square

    def tendency(projected, state):
        term_list = [projected[number] + coupling * wave_vector[number] * state[1] - viscous_rate * square_wave * state[number] for number in range(3)]
        term_list[0] = term_list[0] - shear_rate * state[1]
        return jnp.stack(term_list)

    tendencies = jnp.stack([tendency(proj_real, remeshed[:, 0]), tendency(proj_imag, remeshed[:, 1])], axis=1)
    new_accumulator = (-5.0 / 9.0) * carried + step[0] * tendencies
    new_velocity = remeshed + (15.0 / 16.0) * new_accumulator
    stress = jnp.sum(remeshed[0, 0] * remeshed[1, 0] + remeshed[0, 1] * remeshed[1, 1], axis=(1, 2)) / (NY * NZ)
    energy = jnp.sum(remeshed * remeshed, axis=(0, 1))
    dissipation = 2.0 * viscous_rate * jnp.sum(square_wave * energy, axis=(1, 2)) / (NY * NZ)
    return new_velocity, new_accumulator, jnp.stack([stress, dissipation])
```

```python
import jax
import jax.numpy as jnp
import numpy as np
from jax import lax
from jax.experimental import pallas as pl
from jax.experimental.pallas import tpu as pltpu
from jax.sharding import PartitionSpec as P

NX = 256
NY = 256
NZ = 256


def tables(period):
    positions = np.arange(period)
    angles = (positions[:, None] * positions[None, :] % period) * (2.0 * np.pi / period)
    factor = 1.0 / np.sqrt(period)
    return np.cos(angles) * factor, np.sin(angles) * factor


def dot(formula, first, second):
    return jnp.einsum(
        formula, first, second, precision=lax.Precision.HIGH, preferred_element_type=jnp.float32
    )


def const(table):
    return jnp.asarray(np.ascontiguousarray(table), jnp.float32)


def make_tables(half_x, rows, cols):
    cos_x, sin_x = tables(NX)
    cos_y, sin_y = tables(NY)
    cos_z, sin_z = tables(NZ)
    block_y = NY // cols
    block_z = NZ // rows
    width_z = NZ // cols
    width_x = half_x // rows
    cy = cos_y.reshape(NY, cols, 1, block_y)
    sy = sin_y.reshape(NY, cols, 1, block_y)
    inv_y = np.stack([np.concatenate([cy, sy], 2), np.concatenate([-sy, cy], 2)])
    inv_y = inv_y.reshape(2 * NY, cols, 2 * block_y)
    cz = cos_z.reshape(rows, block_z, cols, width_z)
    sz = sin_z.reshape(rows, block_z, cols, width_z)
    inv_z = np.stack([cz, sz], 2)
    weight = np.where(np.arange(half_x) == 0, 1.0, 2.0)
    inv_x = np.stack([cos_x[:, :half_x] * weight, -sin_x[:, :half_x] * weight], 1)
    cx = cos_x[:half_x].reshape(rows, width_x, NX)
    sx = sin_x[:half_x].reshape(rows, width_x, NX)
    fwd_x = np.stack([cx, -sx], 1)
    cz = cos_z.reshape(cols, width_z, rows, block_z)
    sz = sin_z.reshape(cols, width_z, rows, block_z)
    fwd_z = np.stack([cz, sz], 2)
    cy = cos_y.reshape(cols, block_y, NY)
    sy = sin_y.reshape(cols, block_y, NY)
    fwd_y = np.concatenate(
        [np.concatenate([cy, -sy], 2), np.concatenate([sy, cy], 2)], 1
    )
    return [const(table) for table in (inv_y, inv_z, inv_x, fwd_x, fwd_z, fwd_y)]


def exchange(field, axis):
    return lax.all_to_all(field, axis, split_axis=0, concat_axis=0, tiled=True)


def to_grid(smooth, inv_y, inv_z, inv_x):
    part = dot("abk,kqj->qabj", smooth, inv_y)
    part = exchange(part, "col")
    half = part.shape[-1] // 2
    turned = jnp.concatenate([-part[..., half:], part[..., :half]], -1)
    part = dot("rzuhb,uhabk->razk", inv_z, jnp.stack([part, turned]))
    part = exchange(part, "row")
    rows, width, block_z, lanes = part.shape
    part = part.reshape(rows * width, block_z, lanes)
    mid = block_z // 2
    packed = jnp.stack(
        [
            jnp.concatenate([piece[:, :mid], piece[:, mid:]], -1)
            for piece in (part[..., :half], part[..., half:])
        ]
    )
    return dot("xtk,tkmj->xmj", inv_x, packed)


def to_modes(grid, fwd_x, fwd_z, fwd_y):
    part = exchange(dot("rtax,xmj->rtamj", fwd_x, grid), "row")
    half = part.shape[-1] // 2
    part = jnp.concatenate(
        [
            jnp.concatenate([part[:, t, ..., :half], part[:, t, ..., half:]], 2)
            for t in range(2)
        ],
        -1,
    )
    turned = jnp.concatenate([part[..., half:], -part[..., :half]], -1)
    part = dot("qbuhz,uhazk->qabk", fwd_z, jnp.stack([part, turned]))
    part = exchange(part, "col")
    return dot("habk,hkj->abj", part, fwd_y)


def geometry(base, real, shape):
    index_x = base[0] + pl.program_id(0)
    kx = index_x.astype(jnp.float32)
    iz = lax.broadcasted_iota(jnp.int32, shape, 0) + base[1]
    iz = jnp.where(2 * iz < NZ, iz, iz - NZ)
    iy = lax.broadcasted_iota(jnp.int32, shape, 1)
    iy = jnp.where(2 * iy < NY, iy, iy - NY)
    k0 = jnp.full(shape, kx, jnp.float32)
    k1 = iy.astype(jnp.float32) - real[4] * k0
    k2 = iz.astype(jnp.float32)
    ksq = k0 * k0 + k1 * k1 + k2 * k2
    inv = 1.0 / jnp.maximum(ksq, 1.0)
    keep = (3 * jnp.abs(iz) < NZ) & (3 * jnp.abs(iy) < NY) & (3.0 * k0 < float(NX))
    mask = jnp.where(keep, 1.0, 0.0)
    return (k0, k1, k2), ksq, inv, mask


def project(field, k, inv):
    along = (k[0] * field[0] + k[1] * field[1] + k[2] * field[2]) * inv
    return [field[c] - k[c] * along for c in range(3)]


def first_kernel(amount, base, real, vel, smooth, sums):
    shape = vel.shape[3:]
    full_y = shape[1]
    k, ksq, inv, mask = geometry(base, real, shape)
    shift = amount[pl.program_id(0)]
    v = [[pltpu.roll(vel[c, p, 0], shift, 1) for p in range(2)] for c in range(3)]
    stress = v[0][0] * v[1][0] + v[0][1] * v[1][1]
    energy = sum(v[c][p] * v[c][p] for c in range(3) for p in range(2))
    sums[0, 0:1] = jnp.sum(stress, axis=0, keepdims=True)
    sums[0, 1:2] = jnp.sum(ksq * energy, axis=0, keepdims=True)
    for p in range(2):
        out = project([v[c][p] for c in range(3)], k, inv)
        for c in range(3):
            smooth[c, 0, :, p * full_y : (p + 1) * full_y] = mask * out[c]


def last_kernel(amount, base, real, vel, acc, d0, d1, t01, t02, t12, new_vel, new_acc):
    shape = vel.shape[3:]
    full_y = shape[1]
    k, ksq, inv, mask = geometry(base, real, shape)
    shift = amount[pl.program_id(0)]
    viscosity, shear, step = real[0], real[1], real[3]
    coupling = 2.0 * shear * k[0] * inv
    for p in range(2):
        v = [pltpu.roll(vel[c, p, 0], shift, 1) for c in range(3)]
        old = [pltpu.roll(acc[c, p, 0], shift, 1) for c in range(3)]
        sign = mask if p == 0 else -mask
        other = slice((1 - p) * full_y, (2 - p) * full_y)
        e0, e1, e01, e02, e12 = [ref[0, :, other] for ref in (d0, d1, t01, t02, t12)]
        hat = [
            sign * (k[0] * e0 + k[1] * e01 + k[2] * e02),
            sign * (k[0] * e01 + k[1] * e1 + k[2] * e12),
            sign * (k[0] * e02 + k[1] * e12),
        ]
        hat = project(hat, k, inv)
        for c in range(3):
            rate = hat[c] + coupling * k[c] * v[1] - viscosity * ksq * v[c]
            if c == 0:
                rate = rate - shear * v[1]
            total = (-5.0 / 9.0) * old[c] + step * rate
            new_acc[c, p, 0] = total
            new_vel[c, p, 0] = v[c] + (15.0 / 16.0) * total


def body(velocity, accumulator, remesh_flag, remesh_shift, viscosity, shear, clock, step):
    rows = lax.axis_size("row")
    cols = lax.axis_size("col")
    _, _, width_x, width_z, full_y = velocity.shape
    amount = jnp.mod(-(remesh_flag * remesh_shift), full_y).astype(jnp.int32)
    base = jnp.stack(
        [lax.axis_index("row") * width_x, lax.axis_index("col") * width_z]
    ).astype(jnp.int32)
    real = jnp.concatenate([viscosity, shear, clock, step, shear * clock])
    state_spec = pl.BlockSpec((3, 2, 1, width_z, full_y), lambda i, *_: (0, 0, i, 0, 0))
    mode_spec = pl.BlockSpec((1, width_z, 2 * full_y), lambda i, *_: (i, 0, 0))
    params = pltpu.CompilerParams(
        dimension_semantics=("arbitrary",), vmem_limit_bytes=48 * 1024 * 1024
    )
    smooth, sums = pl.pallas_call(
        first_kernel,
        grid_spec=pltpu.PrefetchScalarGridSpec(
            num_scalar_prefetch=3,
            grid=(width_x,),
            in_specs=[state_spec],
            out_specs=[
                pl.BlockSpec((3, 1, width_z, 2 * full_y), lambda i, *_: (0, i, 0, 0)),
                pl.BlockSpec((1, 2, full_y), lambda i, *_: (i, 0, 0)),
            ],
        ),
        out_shape=[
            jax.ShapeDtypeStruct((3, width_x, width_z, 2 * full_y), jnp.float32),
            jax.ShapeDtypeStruct((width_x, 2, full_y), jnp.float32),
        ],
        compiler_params=params,
    )(amount, base, real, velocity)
    totals = lax.psum(jnp.sum(sums, axis=-1), "col")
    inv_y, inv_z, inv_x, fwd_x, fwd_z, fwd_y = make_tables(width_x * rows, rows, cols)
    u, v, w = [to_grid(smooth[c], inv_y, inv_z, inv_x) for c in range(3)]
    products = (u * u - w * w, v * v - w * w, u * v, u * w, v * w)
    modes = [to_modes(product, fwd_x, fwd_z, fwd_y) for product in products]
    new_velocity, new_accumulator = pl.pallas_call(
        last_kernel,
        grid_spec=pltpu.PrefetchScalarGridSpec(
            num_scalar_prefetch=3,
            grid=(width_x,),
            in_specs=[state_spec] * 2 + [mode_spec] * 5,
            out_specs=[state_spec] * 2,
        ),
        out_shape=[jax.ShapeDtypeStruct(velocity.shape, jnp.float32)] * 2,
        compiler_params=params,
    )(amount, base, real, velocity, accumulator, *modes)
    stress = totals[:, 0] / (NY * NZ)
    dissipation = 2.0 * viscosity[0] * totals[:, 1] / (NY * NZ)
    return new_velocity, new_accumulator, jnp.stack([stress, dissipation])


def solution(mesh):
    state = P(None, None, "row", "col", None)
    in_specs = (state, state, P("row"), P("row"), P(), P(), P(), P())
    out_specs = (state, state, P(None, "row"))
    return jax.shard_map(
        body, mesh=mesh, in_specs=in_specs, out_specs=out_specs, check_vma=False
    )
```
